32 devices in a mesh: parts: 2 (over y), slab: 4 (over z), blk: 2 (over x), head: 2 (over core).
Axes of the slice: x: 2, y: 2, z: 4, core: 2. Of those that a mesh axis runs over, the one named last changes fastest.
Arguments:
- features: bfloat16 [4096, 512], P(('parts', 'slab', 'blk')), parts along dimension 0, may hold values from -16 to 16
- cotangent: bfloat16 [4096, 512], P(('parts', 'slab', 'blk')), parts along dimension 0, may hold values from -6 to 6
- w_query: bfloat16 [512, 512], P(None, 'head'), may hold values from -0.25 to 0.25
- w_key: bfloat16 [512, 512], P(None, 'head'), may hold values from -0.25 to 0.25
- w_value: bfloat16 [512, 512], P(None, 'head'), may hold values from -0.25 to 0.25
- w_out: bfloat16 [512, 512], P('head'), may hold values from -0.25 to 0.25
- adjacency: int32 [32, 3], P(('parts', 'slab', 'blk')), parts along dimension 0, may hold values from 0 to 1, as said below
- partner: int32 [3, 32], P(None, ('parts', 'slab', 'blk')), parts along dimension 1, may hold values from 0 to 15, as said below
- node_order: int32 [4096], P(('parts', 'slab', 'blk')), parts along dimension 0, may hold values from 0 to 255, as said below
Outputs:
- grad_input: bfloat16 [4096, 512], P(('parts', 'slab', 'blk'), 'head'), parts along dimension 0
The draws below stay inside these ranges and needn't reach their ends.
There are 2 independent parts, one for each index of `parts`. The reference program is written for one: setup_inputs(seed, part) draws one part's arguments, and reference() takes and returns one part's arrays. A program takes and returns all parts, laid end to end along the dimension named above; an argument that names none is the same for every part. Nothing has to cross between parts.
Inputs may be any that keep to these rules, and one draw needn't show every extreme that they name: `adjacency`: column 1 (the block itself) is always 1. partner[m, g] is the block at the same position among its device's 2 blocks, on the device of the same blk index in another slab; partner[m, partner[m, g]] = g. Of the 3 * 2 (matching, block) pairs of one device, at most 2 have their partner in one slab, and on every device exactly 2 do for some slab. `node_order`: within each device's 2 * 128 positions, a permutation of the device's rows.
All inputs are finite; a program needn't handle non-finite values.
Results may differ from the reference program's by a relative error of at most 0.013.
The reference program's roundings to bfloat16 on the way count: a program that leaves them out, or rounds other values in their place, can miss the bound.
Values may be sent and summed in bfloat16 or wider, within the bound.
A program may use at most 64 MiB of HBM per device.

```python
import jax
import jax.numpy as jnp
from jax import lax

D = 512
HEADS = 8
BLOCK = 128
BPD = 2
HEAD_DIM = 64
TOTAL_BLOCKS = 16
NODES = 2048
CAP = 2
N_SLAB = 4
N_BLK = 2


def draw_features(key, part):
    return jnp.clip(jax.random.normal(key, (NODES, D), jnp.float32), -6.0, 6.0).astype(jnp.bfloat16)


def draw_adjacency(key, part):
    bits = jax.random.randint(jax.random.fold_in(key, 7), (TOTAL_BLOCKS, 3), 0, 2, dtype=jnp.int32)
    return bits.at[:, 1].set(1)


def draw_node_order(key, part):
    device_count = NODES // (BPD * BLOCK)
    device_keys = jax.random.split(jax.random.fold_in(key, 5), device_count)
    orders = jax.vmap(lambda one_key: jax.random.permutation(one_key, BPD * BLOCK))(device_keys)
    return orders.reshape(NODES).astype(jnp.int32)


def draw_partner(key, part):
    item_count = 3 * BPD

    def column_codes(column_key):
        codes = jax.random.permutation(column_key, N_SLAB - 1).astype(jnp.int32) + 1
        repeated = jnp.repeat(codes, CAP, total_repeat_length=(N_SLAB - 1) * CAP)[:item_count]
        shuffle = jax.random.permutation(jax.random.fold_in(column_key, 1), item_count)
        return repeated[shuffle]
    codes = jax.vmap(column_codes)(jax.random.split(jax.random.fold_in(key, 11), N_BLK))
    codes = jnp.transpose(codes.reshape(N_BLK, 3, BPD), (1, 0, 2))
    label_keys = jax.random.split(jax.random.fold_in(key, 12), N_BLK)
    labels = jax.vmap(lambda one_key: jax.random.permutation(one_key, N_SLAB))(label_keys)
    labels = labels.astype(jnp.int32).reshape(N_BLK, N_SLAB)
    unlabel = jnp.argsort(labels, axis=-1).astype(jnp.int32)
    unlabel = jnp.broadcast_to(unlabel[None], (3, N_BLK, N_SLAB))
    target = jnp.bitwise_xor(labels[None, :, :, None], codes[:, :, None, :])
    slab_of = jnp.take_along_axis(unlabel, target.reshape(3, N_BLK, N_SLAB * BPD), axis=2)
    slab_of = slab_of.reshape(3, N_BLK, N_SLAB, BPD)
    column = jnp.arange(N_BLK, dtype=jnp.int32)[None, :, None, None]
    position = jnp.arange(BPD, dtype=jnp.int32)[None, None, None, :]
    global_id = (slab_of * N_BLK + column) * BPD + position
    return jnp.transpose(global_id, (0, 2, 1, 3)).reshape(3, TOTAL_BLOCKS).astype(jnp.int32)


def shard_levels(rng, shape, cuts, low, largest):
    def one(dim, parts):
        steps = jax.random.uniform(jax.random.fold_in(jax.random.fold_in(rng, 6), dim), (parts,), jnp.float32, low / len(cuts), largest / len(cuts))
        return jnp.repeat(jnp.exp(steps), shape[dim] // parts).reshape((-1,) + (1,) * (len(shape) - dim - 1))

    gain = one(*cuts[0])
    for cut in cuts[1:]:
        gain = gain * one(*cut)
    return gain


def scatter_about(stream_key, dims, width, most, cuts=(), held_as=jnp.bfloat16):
    level = shard_levels(stream_key, dims, cuts, -0.22, 0.18) if cuts else 1.0
    values = jax.random.normal(stream_key, dims, jnp.float32) * width * level
    return jnp.minimum(jnp.maximum(values, -most), most).astype(held_as)


def setup_inputs(seed: int = 0, part: int = 0) -> dict:
    streams_of = jax.random.split(jax.random.key(seed), 10)
    own_keys = jax.random.split(jax.random.fold_in(streams_of[9], part), 10)
    features = draw_features(jax.random.fold_in(jax.random.fold_in(streams_of[9], part), 71), part)
    cotangent = scatter_about(own_keys[1], (NODES, D), 1.0, 6.0, ((0, 8),))
    w_query = scatter_about(streams_of[2], (D, D), D ** -0.5, 0.25, ((1, 2),))
    w_key = scatter_about(streams_of[3], (D, D), D ** -0.5, 0.25, ((1, 2),))
    w_value = scatter_about(streams_of[4], (D, D), D ** -0.5, 0.25, ((1, 2),))
    w_out = scatter_about(streams_of[5], (D, D), D ** -0.5, 0.25, ((0, 2),))
    adjacency = draw_adjacency(jax.random.fold_in(jax.random.fold_in(streams_of[9], part), 71), part)
    partner = draw_partner(jax.random.fold_in(jax.random.fold_in(streams_of[9], part), 71), part)
    node_order = draw_node_order(jax.random.fold_in(jax.random.fold_in(streams_of[9], part), 71), part)
    return dict(features=features, cotangent=cotangent, w_query=w_query, w_key=w_key, w_value=w_value, w_out=w_out, adjacency=adjacency, partner=partner, node_order=node_order)


def reference(features, cotangent, w_query, w_key, w_value, w_out, adjacency, partner, node_order):
    device_rows = BPD * BLOCK
    cycle_len = N_BLK * BPD
    score_scale = HEAD_DIM ** -0.5
    source_rows = (jnp.arange(NODES, dtype=jnp.int32) // device_rows) * device_rows + node_order.astype(jnp.int32)
    blocked_input = features[source_rows]
    blocked_grad = cotangent[source_rows]
    query_rows = jnp.dot(blocked_input, w_query, preferred_element_type=jnp.float32).astype(jnp.bfloat16)
    key_rows = jnp.dot(blocked_input, w_key, preferred_element_type=jnp.float32).astype(jnp.bfloat16)
    value_rows = jnp.dot(blocked_input, w_value, preferred_element_type=jnp.float32).astype(jnp.bfloat16)
    grad_mix = jnp.dot(blocked_grad, jnp.transpose(w_out), preferred_element_type=jnp.float32).astype(jnp.bfloat16)
    block_shape = (TOTAL_BLOCKS, BLOCK, HEADS, HEAD_DIM)
    key_blocks = key_rows.reshape(block_shape)
    value_blocks = value_rows.reshape(block_shape)
    block_ids = jnp.arange(TOTAL_BLOCKS, dtype=jnp.int32)
    slab_base = (block_ids // cycle_len) * cycle_len
    offsets = jnp.arange(3, dtype=jnp.int32) - 1
    near_ids = slab_base[:, None] + (block_ids[:, None] % cycle_len + offsets[None, :]) % cycle_len
    chosen = jnp.concatenate([near_ids, jnp.transpose(partner).astype(jnp.int32)], axis=1)
    switch = jnp.concatenate([adjacency > 0, jnp.ones((TOTAL_BLOCKS, 3), dtype=bool)], axis=1)
    groups = TOTAL_BLOCKS // BPD

    def grouped(source):
        return source.reshape((groups, BPD) + source.shape[1:])

    def visit(totals, pieces):
        grad_keys, grad_values = totals
        queries, upstream, picked, wanted = pieces
        queries = queries.astype(jnp.float32)
        upstream = upstream.astype(jnp.float32)
        keys_here = key_blocks[picked].reshape(BPD, 6 * BLOCK, HEADS, HEAD_DIM).astype(jnp.float32)
        values_here = value_blocks[picked].reshape(BPD, 6 * BLOCK, HEADS, HEAD_DIM).astype(jnp.float32)
        scores = jnp.einsum('gqhd,gkhd->ghqk', queries, keys_here) * score_scale
        keys_on = jnp.repeat(wanted, BLOCK, axis=1)
        scores = jnp.where(keys_on[:, None, None, :], scores, -jnp.inf)
        row_peak = jnp.max(scores, axis=-1, keepdims=True)
        row_total = jnp.log(jnp.sum(jnp.exp(scores - row_peak), axis=-1, keepdims=True)) + row_peak
        attention = jnp.exp(scores - row_total)
        attention_low = lax.optimization_barrier(attention.astype(jnp.bfloat16)).astype(jnp.float32)
        mixed_rows = jnp.einsum('ghqk,gkhd->gqhd', attention_low, values_here)
        row_dot = jnp.transpose(jnp.sum(upstream * mixed_rows, axis=-1), (0, 2, 1))
        grad_attention = jnp.einsum('gqhd,gkhd->ghqk', upstream, values_here)
        grad_scores = attention * (grad_attention - row_dot[..., None])
        grad_scores = lax.optimization_barrier(grad_scores.astype(jnp.bfloat16)).astype(jnp.float32)
        grad_query = score_scale * jnp.einsum('ghqk,gkhd->gqhd', grad_scores, keys_here)
        key_terms = score_scale * jnp.einsum('ghqk,gqhd->gkhd', grad_scores, queries)
        value_terms = jnp.einsum('ghqk,gqhd->gkhd', attention_low, upstream)
        flat_ids = picked.reshape(-1)
        grad_keys = grad_keys.at[flat_ids].add(key_terms.reshape(BPD * 6, BLOCK, HEADS, HEAD_DIM))
        grad_values = grad_values.at[flat_ids].add(value_terms.reshape(BPD * 6, BLOCK, HEADS, HEAD_DIM))
        return (grad_keys, grad_values), grad_query

    start = (jnp.zeros(block_shape, jnp.float32), jnp.zeros(block_shape, jnp.float32))
    pieces = (grouped(query_rows.reshape(block_shape)), grouped(grad_mix.reshape(block_shape)), grouped(chosen), grouped(switch))
    (grad_keys, grad_values), grad_queries = lax.scan(visit, start, pieces)
    grad_query = grad_queries.reshape(NODES, D).astype(jnp.bfloat16)
    grad_key = grad_keys.reshape(NODES, D).astype(jnp.bfloat16)
    grad_value = grad_values.reshape(NODES, D).astype(jnp.bfloat16)
    branch = jnp.dot(grad_query, jnp.transpose(w_query), preferred_element_type=jnp.float32)
    branch = branch + jnp.dot(grad_key, jnp.transpose(w_key), preferred_element_type=jnp.float32)
    branch = branch + jnp.dot(grad_value, jnp.transpose(w_value), preferred_element_type=jnp.float32)
    grad_input = jnp.zeros((NODES, D), jnp.float32).at[source_rows].set(branch)
    return grad_input.astype(jnp.bfloat16)
```

```python
import functools

import jax
import jax.numpy as jnp
from jax import lax
from jax.experimental import pallas as pl
from jax.experimental.pallas import tpu as pltpu
from jax.sharding import PartitionSpec as P

HEAD_DIM = 64
OFF = -1e30
NT = (((1,), (1,)), ((), ()))
TN = (((0,), (0,)), ((), ()))
F32, BF16 = jnp.float32, jnp.bfloat16
MESH = pl.DeviceIdType.MESH


def mm(a, b):
    return jnp.dot(a, b, preferred_element_type=F32)


def mm_nt(a, b):
    return lax.dot_general(a, b, NT, preferred_element_type=F32)


def kernel(
    n, nb,
    feat, cot, w_q, w_k, w_v, w_o, adj, part, order, out,
    perm, own_x, own_c, rx, rc, k_own, v_own, kt_own, qm_own, gm_own,
    kt_far, qm_far, s_loc, g_loc, s_far, g_far, s_back, peak, stat, stat_far,
    dq, dk, dv, give, take,
    x_send, x_recv, xf_send, xf_recv, c_send, c_recv, cf_send, cf_recv,
    t_send, t_recv, h_send, h_recv,
):
    rows, width = feat.shape
    half = width // 2
    cols = w_q.shape[1]
    heads = cols // HEAD_DIM
    block = rows // 2
    scale = HEAD_DIM ** -0.5
    h, slab, x = (lax.axis_index(a) for a in ("head", "slab", "blk"))
    behind, ahead = {"blk": lax.rem(x + nb - 1, nb)}, {"blk": lax.rem(x + 1, nb)}
    twin = {"head": 1 - h}

    def onward(d):
        return {"slab": lax.rem(slab + d, n)}

    def each(f):
        if n <= 4:
            for d in sorted(range(1, n), key=lambda d: (min(d, n - d), d)):
                f(d)
        else:
            lax.fori_loop(1, n, lambda d, c: (f(d), c)[1], 0)

    barrier = pltpu.get_barrier_semaphore()

    def greet(where):
        pl.semaphore_signal(barrier, inc=1, device_id=where, device_id_type=MESH)

    greet(behind)
    greet(ahead)
    greet(twin)
    each(lambda d: greet(onward(d)))

    def copy(src, dst, send, recv, where):
        return pltpu.make_async_remote_copy(
            src_ref=src, dst_ref=dst, send_sem=send, recv_sem=recv,
            device_id=where, device_id_type=MESH,
        )

    low, high = pl.ds(0, block), pl.ds(block, block)

    def near_copies(own, far, send, recv):
        return (
            copy(own.at[h, low], far.at[0, h, high], send.at[n], recv.at[n], behind),
            copy(own.at[h, high], far.at[0, h, low], send.at[0], recv.at[0], ahead),
        )

    def slab_copy(own, far, send, recv, d):
        return copy(own.at[h], far.at[d, h], send.at[d], recv.at[d], onward(d))

    def twin_copy(far, send, recv, i):
        return copy(far.at[i, h], far.at[i, h], send.at[i], recv.at[i], twin)

    x_near = functools.partial(near_copies, own_x, rx, x_send, x_recv)
    c_near = functools.partial(near_copies, own_c, rc, c_send, c_recv)
    x_slab = functools.partial(slab_copy, own_x, rx, x_send, x_recv)
    c_slab = functools.partial(slab_copy, own_c, rc, c_send, c_recv)
    x_twin = functools.partial(twin_copy, rx, xf_send, xf_recv)
    c_twin = functools.partial(twin_copy, rc, cf_send, cf_recv)

    def stat_near():
        return (
            copy(stat.at[0], stat_far.at[0, 1], t_send.at[n], t_recv.at[n], behind),
            copy(stat.at[1], stat_far.at[0, 0], t_send.at[0], t_recv.at[0], ahead),
        )

    def stat_slab(d):
        return copy(stat, stat_far.at[d], t_send.at[d], t_recv.at[d], onward(d))

    hot = lax.broadcasted_iota(jnp.int32, (rows, rows), 0) == order[...]
    perm[...] = jnp.where(hot, 1.0, 0.0).astype(BF16)
    x_all = lax.dot_general(perm[...], feat[...], TN, preferred_element_type=F32).astype(BF16)
    own_x[0] = x_all[:, :half]
    own_x[1] = x_all[:, half:]
    pl.semaphore_wait(barrier, n + 2)
    for c in x_near():
        c.start()
    each(lambda d: x_slab(d).start())

    c_all = lax.dot_general(perm[...], cot[...], TN, preferred_element_type=F32).astype(BF16)
    own_c[0] = c_all[:, :half]
    own_c[1] = c_all[:, half:]

    lane_head = lax.broadcasted_iota(jnp.int32, (1, cols), 1) // HEAD_DIM
    masks = [jnp.where(lane_head == i, 1.0, 0.0).astype(BF16) for i in range(heads)]

    def masked(value, b):
        part_rows = value[b * block:(b + 1) * block]
        return jnp.concatenate([part_rows * mask for mask in masks], axis=0)

    def weight_flag(flag):
        return jnp.where(flag > 0, 1.0, 0.0).astype(F32)

    def far_weight(i, b):
        if isinstance(i, int) and i == 0:
            return weight_flag(adj[0, 0] if b == 0 else adj[1, 2])
        source = lax.rem(slab + n - i, n)
        total = jnp.float32(0.0)
        for m in range(3):
            total = total + jnp.where(lax.div(part[m, b], 2 * nb) == source, 1.0, 0.0)
        return total

    def local_weight(kb, qb):
        if kb == qb:
            return jnp.float32(1.0)
        return weight_flag(adj[0, 2] if qb == 0 else adj[1, 0])

    def bias(w):
        return jnp.where(w > 0.0, 0.0, OFF).astype(F32)

    q_all = (mm(x_all, w_q[...]).astype(BF16) * scale).astype(BF16)
    k_all = mm(x_all, w_k[...])
    k_own[...] = k_all.astype(BF16)
    kt_own[...] = k_all.T.astype(BF16)
    v_own[...] = mm(x_all, w_v[...]).astype(BF16)
    g_all = mm_nt(c_all, w_o[...]).astype(BF16)
    for b in range(2):
        qm_own[b] = masked(q_all, b)
        gm_own[b] = masked(g_all, b)
    for c in c_near():
        c.start()
    each(lambda d: c_slab(d).start())
    for b in range(2):
        s = mm_nt(k_own[...], qm_own[b])
        s_loc[b] = s
        g_loc[b] = mm_nt(v_own[...], gm_own[b])
        top = [
            jnp.max(s[kb * block:(kb + 1) * block], axis=0, keepdims=True)
            + bias(local_weight(kb, b))
            for kb in range(2)
        ]
        peak[b] = jnp.maximum(top[0], top[1])

    def forward_slot(i):
        x0, x1 = rx[i, 0], rx[i, 1]

        def project(w):
            return mm(x0, w[:half, :]) + mm(x1, w[half:, :])

        q = (project(w_q).astype(BF16) * scale).astype(BF16)
        k32 = project(w_k)
        k = k32.astype(BF16)
        kt_far[i] = k32.T.astype(BF16)
        v = project(w_v).astype(BF16)
        for b in range(2):
            here = slice(b * block, (b + 1) * block)
            qm = masked(q, b)
            qm_far[i, b] = qm
            s = mm_nt(k[here], qm_own[b])
            s_far[i, b] = s
            g_far[i, b] = mm_nt(v[here], gm_own[b])
            s_back[i, b] = mm_nt(k_own[here, :], qm)
            top = jnp.max(s, axis=0, keepdims=True) + bias(far_weight(i, b))
            peak[b] = jnp.maximum(peak[b], top)

    for c in x_near():
        c.wait_recv()
    x_twin(0).start()
    x_twin(0).wait_recv()
    forward_slot(0)

    def take_x(d):
        x_slab(d).wait_recv()
        x_twin(d).start()
        x_twin(d).wait_recv()
        forward_slot(d)

    each(take_x)

    for b in range(2):
        qcols = slice(b * block, (b + 1) * block)
        top = peak[b]

        def expo(ref, at, w, total):
            e = jnp.exp(ref[at] + (bias(w) - top))
            ref[at] = e
            return total + w * jnp.sum(e, axis=0, keepdims=True)

        def loc(kb):
            return (b, slice(kb * block, (kb + 1) * block))

        total = jnp.zeros((1, heads * block), F32)
        for kb in range(2):
            total = expo(s_loc, loc(kb), local_weight(kb, b), total)
        total = expo(s_far, (0, b), far_weight(0, b), total)
        stat[b, 0:1] = total

        def far_expo(d):
            stat[b, 0:1] = expo(s_far, (d, b), far_weight(d, b), stat[b, 0:1])

        each(far_expo)
        total = stat[b, 0:1]
        inverse = 1.0 / total

        def weigh(sref, gref, at, w):
            p = sref[at] * (w * inverse)
            sref[at] = p
            low_p = p.astype(BF16).astype(F32)
            return jnp.sum(low_p * gref[at], axis=0, keepdims=True)

        dot = weigh(s_far, g_far, (0, b), far_weight(0, b))
        for kb in range(2):
            dot = dot + weigh(s_loc, g_loc, loc(kb), local_weight(kb, b))
        stat[b, 1:2] = dot

        def far_weigh(d):
            stat[b, 1:2] = stat[b, 1:2] + weigh(s_far, g_far, (d, b), far_weight(d, b))

        each(far_weigh)
        stat[b, 0:1] = top + jnp.log(total)
        flag = weight_flag(adj[0, 0] if b == 0 else adj[1, 2])
        stat[b, 2:3] = jnp.zeros((1, heads * block), F32) + flag
        stat[b, 3:8] = jnp.zeros((5, heads * block), F32)
    for c in stat_near():
        c.start()
    each(lambda d: stat_slab(d).start())

    for b in range(2):
        qcols = slice(b * block, (b + 1) * block)
        dot = stat[b, 1:2]
        p = s_loc[b]
        ds = (p * (g_loc[b] - dot)).astype(BF16)
        p_low = p.astype(BF16)
        if b == 0:
            dv[...] = mm(p_low, gm_own[b])
            dk[...] = mm(ds, qm_own[b])
        else:
            dv[...] += mm(p_low, gm_own[b])
            dk[...] += mm(ds, qm_own[b])
        for i in range(heads):
            hd = slice(i * HEAD_DIM, (i + 1) * HEAD_DIM)
            dq[hd, qcols] = mm(kt_own[hd, :], ds[:, i * block:(i + 1) * block])

        def query_grad(i):
            ds_i = (s_far[i, b] * (g_far[i, b] - stat[b, 1:2])).astype(BF16)
            for j in range(heads):
                hd = slice(j * HEAD_DIM, (j + 1) * HEAD_DIM)
                dq[hd, qcols] += mm(kt_far[i, hd, qcols], ds_i[:, j * block:(j + 1) * block])

        query_grad(0)
        each(query_grad)

    def backward_slot(i):
        c0, c1 = rc[i, 0], rc[i, 1]
        g = (mm_nt(c0, w_o[:, :half]) + mm_nt(c1, w_o[:, half:])).astype(BF16)
        for b in range(2):
            here = slice(b * block, (b + 1) * block)
            gm = masked(g, b)
            row_total = stat_far[i, b, 0:1]
            dot = stat_far[i, b, 1:2]
            if isinstance(i, int) and i == 0:
                w = stat_far[i, b, 2:3]
            else:
                w = jnp.zeros((1, heads * block), F32) + far_weight(i, b)
            p = jnp.exp(s_back[i, b] - jnp.where(w > 0.0, row_total, -OFF)) * w
            gp = mm_nt(v_own[here, :], gm)
            ds = (p * (gp - dot)).astype(BF16)
            dv[here, :] += mm(p.astype(BF16), gm)
            dk[here, :] += mm(ds, qm_far[i, b])

    for c in c_near():
        c.wait_recv()
    c_twin(0).start()
    c_twin(0).wait_recv()
    for c in stat_near():
        c.wait_recv()
    backward_slot(0)

    def take_c(d):
        c_slab(d).wait_recv()
        c_twin(d).start()
        c_twin(d).wait_recv()
        stat_slab(d).wait_recv()
        backward_slot(d)

    each(take_c)

    dq_low = (dq[...].T * scale).astype(BF16)
    dk_low, dv_low = dk[...].astype(BF16), dv[...].astype(BF16)

    def share(which):
        at = pl.ds(pl.multiple_of(which * half, half), half)
        return mm_nt(dq_low, w_q[at, :]) + mm_nt(dk_low, w_k[at, :]) + mm_nt(dv_low, w_v[at, :])

    give[...] = share(1 - h).astype(BF16)
    swap = copy(give, take, h_send, h_recv, twin)
    swap.start()
    mine = share(h)
    swap.wait_recv()
    branch = (mine + take[...].astype(F32)).astype(BF16)
    out[...] = mm(perm[...], branch).astype(BF16)

    swap.wait_send()
    for c in (*x_near(), *c_near(), *stat_near(), x_twin(0), c_twin(0)):
        c.wait_send()

    def finish(d):
        for c in (x_slab(d), c_slab(d), stat_slab(d), x_twin(d), c_twin(d)):
            c.wait_send()

    each(finish)


def body(features, cotangent, w_query, w_key, w_value, w_out, adjacency, partner, node_order):
    n, nb = lax.axis_size("slab"), lax.axis_size("blk")
    rows, width = features.shape
    cols = w_query.shape[1]
    half, block = width // 2, rows // 2
    lanes = (cols // HEAD_DIM) * block
    vm, dma = pltpu.VMEM, pltpu.SemaphoreType.DMA
    vmem, smem = (pl.BlockSpec(memory_space=m) for m in (pltpu.VMEM, pltpu.SMEM))
    return pl.pallas_call(
        functools.partial(kernel, n, nb),
        out_shape=jax.ShapeDtypeStruct((rows, half), BF16),
        in_specs=[vmem] * 6 + [smem] * 2 + [vmem],
        out_specs=vmem,
        scratch_shapes=[
            vm((rows, rows), BF16),
            vm((2, rows, half), BF16), vm((2, rows, half), BF16),
            vm((n, 2, rows, half), BF16), vm((n, 2, rows, half), BF16),
            vm((rows, cols), BF16), vm((rows, cols), BF16), vm((cols, rows), BF16),
            vm((2, lanes, cols), BF16), vm((2, lanes, cols), BF16),
            vm((n, cols, rows), BF16), vm((n, 2, lanes, cols), BF16),
            vm((2, rows, lanes), F32), vm((2, rows, lanes), F32),
            vm((n, 2, block, lanes), F32), vm((n, 2, block, lanes), F32),
            vm((n, 2, block, lanes), F32),
            vm((2, 1, lanes), F32), vm((2, 8, lanes), F32), vm((n, 2, 8, lanes), F32),
            vm((cols, rows), F32), vm((rows, cols), F32), vm((rows, cols), F32),
            vm((rows, half), BF16), vm((rows, half), BF16),
        ] + [dma((n + 1,)), dma((n + 1,)), dma((n,)), dma((n,))] * 2
        + [dma((n + 1,)), dma((n + 1,)), dma(()), dma(())],
        compiler_params=pltpu.CompilerParams(
            collective_id=0, has_side_effects=True, vmem_limit_bytes=52 * 1024 * 1024
        ),
    )(
        features, cotangent, w_query, w_key, w_value, w_out,
        adjacency, partner, node_order.reshape(1, rows),
    )


def solution(mesh):
    rows = P(("parts", "slab", "blk"), None)
    in_specs = (
        rows, rows,
        P(None, "head"), P(None, "head"), P(None, "head"), P("head", None),
        rows, P(None, ("parts", "slab", "blk")), P(("parts", "slab", "blk")),
    )
    return jax.shard_map(
        body, mesh=mesh, in_specs=in_specs,
        out_specs=P(("parts", "slab", "blk"), "head"), check_vma=False,
    )
```

```python
import functools

import jax
import jax.numpy as jnp
from jax import lax
from jax.experimental import pallas as pl
from jax.experimental.pallas import tpu as pltpu
from jax.sharding import PartitionSpec as P

HEAD_DIM = 64
OFF = -1e30
NT = (((1,), (1,)), ((), ()))
TN = (((0,), (0,)), ((), ()))
F32, BF16 = jnp.float32, jnp.bfloat16
MESH = pl.DeviceIdType.MESH


def mm(a, b):
    return jnp.dot(a, b, preferred_element_type=F32)


def mm_nt(a, b):
    return lax.dot_general(a, b, NT, preferred_element_type=F32)


def kernel(
    n, nb,
    feat_hbm, cot_hbm, w_q_hbm, w_k_hbm, w_v_hbm, w_o_hbm, adj_hbm, part_hbm, order_hbm, out,
    feat, cot, w_q, w_k, w_v, w_o, adj, part, order, fetch,
    perm, own_x, own_c, rx, rc, k_own, v_own, kt_own, qm_own, gm_own,
    kt_far, qm_far, s_loc, g_loc, s_far, g_far, s_back, peak, stat, stat_far,
    dq, dk, dv, give, take,
    x_send, x_recv, xf_send, xf_recv, c_send, c_recv, cf_send, cf_recv,
    t_send, t_recv, h_send, h_recv, hop_send,
):
    rows, width = feat.shape
    half = width // 2
    cols = w_q.shape[1]
    heads = cols // HEAD_DIM
    block = rows // 2
    scale = HEAD_DIM ** -0.5
    h, slab, x = (lax.axis_index(a) for a in ("head", "slab", "blk"))
    behind, ahead = {"blk": lax.rem(x + nb - 1, nb)}, {"blk": lax.rem(x + 1, nb)}
    twin = {"head": 1 - h}

    def onward(d):
        return {"slab": lax.rem(slab + d, n)}

    line = n == 4
    at_start, at_end = slab == 0, slab == n - 1
    inner = jnp.logical_and(slab > 0, slab < n - 1)

    def each(f):
        if line:
            f(jnp.where(at_start, 3, 1))
            f(jnp.where(inner, 3, 2))
            f(jnp.where(at_start, 1, jnp.where(at_end, 3, 2)))
        elif n <= 4:
            for d in range(1, n):
                f(d)
        else:
            lax.fori_loop(1, n, lambda d, c: (f(d), c)[1], 0)

    def each_direct(f):
        if line:
            f(2)
            pl.when(jnp.logical_not(at_end))(lambda: f(1))
            pl.when(jnp.logical_not(at_start))(lambda: f(3))
        else:
            each(f)

    loads = [
        pltpu.make_async_copy(src, dst, fetch.at[i])
        for i, (src, dst) in enumerate((
            (order_hbm, order), (feat_hbm, feat), (cot_hbm, cot), (w_q_hbm, w_q), (w_k_hbm, w_k),
            (w_v_hbm, w_v), (w_o_hbm, w_o), (adj_hbm, adj), (part_hbm, part),
        ))
    ]
    for load in loads:
        load.start()
    barrier = pltpu.get_barrier_semaphore()

    def greet(where):
        pl.semaphore_signal(barrier, inc=1, device_id=where, device_id_type=MESH)

    greet(behind)
    greet(ahead)
    greet(twin)
    each(lambda d: greet(onward(d)))

    def copy(src, dst, send, recv, where):
        return pltpu.make_async_remote_copy(
            src_ref=src, dst_ref=dst, send_sem=send, recv_sem=recv,
            device_id=where, device_id_type=MESH,
        )

    low, high = pl.ds(0, block), pl.ds(block, block)

    def near_copies(own, far, send, recv):
        return (
            copy(own.at[h, low], far.at[0, h, high], send.at[n], recv.at[n], behind),
            copy(own.at[h, high], far.at[0, h, low], send.at[0], recv.at[0], ahead),
        )

    def slab_copy(own, far, send, recv, d):
        return copy(own.at[h], far.at[d, h], send.at[d], recv.at[d], onward(d))

    def twin_copy(far, send, recv, i):
        return copy(far.at[i, h], far.at[i, h], send.at[i], recv.at[i], twin)

    x_near = functools.partial(near_copies, own_x, rx, x_send, x_recv)
    c_near = functools.partial(near_copies, own_c, rc, c_send, c_recv)
    x_slab = functools.partial(slab_copy, own_x, rx, x_send, x_recv)
    c_slab = functools.partial(slab_copy, own_c, rc, c_send, c_recv)
    x_twin = functools.partial(twin_copy, rx, xf_send, xf_recv)
    c_twin = functools.partial(twin_copy, rc, cf_send, cf_recv)

    def hop_copy(far, recv, k):
        up = slab == n - 2
        slot = jnp.where(up, 3, 1)
        return copy(
            far.at[2, h], far.at[slot, h], hop_send.at[k], recv.at[slot],
            {"slab": jnp.where(up, n - 1, 0)},
        )

    x_hop = functools.partial(hop_copy, rx, x_recv, 0)
    c_hop = functools.partial(hop_copy, rc, c_recv, 1)

    def pass_on(slab_copy_of, hop):
        if line:
            @pl.when(inner)
            def _():
                slab_copy_of(2).wait_recv()
                hop().start()

    def arrive(slab_copy_of, d):
        if line:
            pl.when(jnp.logical_not(jnp.logical_and(inner, d == 2)))(
                lambda: slab_copy_of(d).wait_recv()
            )
        else:
            slab_copy_of(d).wait_recv()

    def stat_near():
        return (
            copy(stat.at[0], stat_far.at[0, 1], t_send.at[n], t_recv.at[n], behind),
            copy(stat.at[1], stat_far.at[0, 0], t_send.at[0], t_recv.at[0], ahead),
        )

    def stat_slab(d):
        return copy(stat, stat_far.at[d], t_send.at[d], t_recv.at[d], onward(d))

    loads[0].wait()
    loads[1].wait()
    hot = lax.broadcasted_iota(jnp.int32, (rows, rows), 0) == order[...]
    perm[...] = jnp.where(hot, 1.0, 0.0).astype(BF16)
    x_all = lax.dot_general(perm[...], feat[...], TN, preferred_element_type=F32).astype(BF16)
    own_x[0] = x_all[:, :half]
    own_x[1] = x_all[:, half:]
    pl.semaphore_wait(barrier, n + 2)
    for c in x_near():
        c.start()
    each_direct(lambda d: x_slab(d).start())

    for load in loads[2:]:
        load.wait()
    c_all = lax.dot_general(perm[...], cot[...], TN, preferred_element_type=F32).astype(BF16)
    own_c[0] = c_all[:, :half]
    own_c[1] = c_all[:, half:]

    lane_head = lax.broadcasted_iota(jnp.int32, (1, cols), 1) // HEAD_DIM
    masks = [jnp.where(lane_head == i, 1.0, 0.0).astype(BF16) for i in range(heads)]

    def masked(value, b):
        part_rows = value[b * block:(b + 1) * block]
        return jnp.concatenate([part_rows * mask for mask in masks], axis=0)

    def weight_flag(flag):
        return jnp.where(flag > 0, 1.0, 0.0).astype(F32)

    def far_weight(i, b):
        if isinstance(i, int) and i == 0:
            return weight_flag(adj[0, 0] if b == 0 else adj[1, 2])
        source = lax.rem(slab + n - i, n)
        total = jnp.float32(0.0)
        for m in range(3):
            total = total + jnp.where(lax.div(part[b, m], 2 * nb) == source, 1.0, 0.0)
        return total

    def local_weight(kb, qb):
        if kb == qb:
            return jnp.float32(1.0)
        return weight_flag(adj[0, 2] if qb == 0 else adj[1, 0])

    def bias(w):
        return jnp.where(w > 0.0, 0.0, OFF).astype(F32)

    q_all = (mm(x_all, w_q[...]).astype(BF16) * scale).astype(BF16)
    k_all = mm(x_all, w_k[...])
    k_own[...] = k_all.astype(BF16)
    kt_own[...] = k_all.T.astype(BF16)
    v_own[...] = mm(x_all, w_v[...]).astype(BF16)
    g_all = mm_nt(c_all, w_o[...]).astype(BF16)
    for b in range(2):
        qm_own[b] = masked(q_all, b)
        gm_own[b] = masked(g_all, b)
    for c in c_near():
        c.start()
    each_direct(lambda d: c_slab(d).start())
    for b in range(2):
        s = mm_nt(k_own[...], qm_own[b])
        s_loc[b] = s
        g_loc[b] = mm_nt(v_own[...], gm_own[b])
        top = [
            jnp.max(s[kb * block:(kb + 1) * block], axis=0, keepdims=True)
            + bias(local_weight(kb, b))
            for kb in range(2)
        ]
        peak[b] = jnp.maximum(top[0], top[1])

    def forward_slot(i):
        x0, x1 = rx[i, 0], rx[i, 1]

        def project(w):
            return mm(x0, w[:half, :]) + mm(x1, w[half:, :])

        q = (project(w_q).astype(BF16) * scale).astype(BF16)
        k32 = project(w_k)
        k = k32.astype(BF16)
        kt_far[i] = k32.T.astype(BF16)
        v = project(w_v).astype(BF16)
        for b in range(2):
            here = slice(b * block, (b + 1) * block)
            qm = masked(q, b)
            qm_far[i, b] = qm
            s = mm_nt(k[here], qm_own[b])
            s_far[i, b] = s
            g_far[i, b] = mm_nt(v[here], gm_own[b])
            s_back[i, b] = mm_nt(k_own[here, :], qm)
            top = jnp.max(s, axis=0, keepdims=True) + bias(far_weight(i, b))
            peak[b] = jnp.maximum(peak[b], top)

    pass_on(x_slab, x_hop)
    for c in x_near():
        c.wait_recv()
    x_twin(0).start()
    x_twin(0).wait_recv()
    forward_slot(0)

    def take_x(d):
        arrive(x_slab, d)
        x_twin(d).start()
        x_twin(d).wait_recv()
        forward_slot(d)

    each(take_x)

    for b in range(2):
        qcols = slice(b * block, (b + 1) * block)
        top = peak[b]

        def expo(ref, at, w, total):
            e = jnp.exp(ref[at] + (bias(w) - top))
            ref[at] = e
            return total + w * jnp.sum(e, axis=0, keepdims=True)

        def loc(kb):
            return (b, slice(kb * block, (kb + 1) * block))

        total = jnp.zeros((1, heads * block), F32)
        for kb in range(2):
            total = expo(s_loc, loc(kb), local_weight(kb, b), total)
        total = expo(s_far, (0, b), far_weight(0, b), total)
        stat[b, 0:1] = total

        def far_expo(d):
            stat[b, 0:1] = expo(s_far, (d, b), far_weight(d, b), stat[b, 0:1])

        each(far_expo)
        total = stat[b, 0:1]
        inverse = 1.0 / total

        def weigh(sref, gref, at, w):
            p = sref[at] * (w * inverse)
            sref[at] = p
            low_p = p.astype(BF16).astype(F32)
            return jnp.sum(low_p * gref[at], axis=0, keepdims=True)

        dot = weigh(s_far, g_far, (0, b), far_weight(0, b))
        for kb in range(2):
            dot = dot + weigh(s_loc, g_loc, loc(kb), local_weight(kb, b))
        stat[b, 1:2] = dot

        def far_weigh(d):
            stat[b, 1:2] = stat[b, 1:2] + weigh(s_far, g_far, (d, b), far_weight(d, b))

        each(far_weigh)
        stat[b, 0:1] = top + jnp.log(total)
        flag = weight_flag(adj[0, 0] if b == 0 else adj[1, 2])
        stat[b, 2:3] = jnp.zeros((1, heads * block), F32) + flag
        stat[b, 3:8] = jnp.zeros((5, heads * block), F32)
    for c in stat_near():
        c.start()
    each(lambda d: stat_slab(d).start())

    for b in range(2):
        qcols = slice(b * block, (b + 1) * block)
        dot = stat[b, 1:2]
        p = s_loc[b]
        ds = (p * (g_loc[b] - dot)).astype(BF16)
        p_low = p.astype(BF16)
        if b == 0:
            dv[...] = mm(p_low, gm_own[b])
            dk[...] = mm(ds, qm_own[b])
        else:
            dv[...] += mm(p_low, gm_own[b])
            dk[...] += mm(ds, qm_own[b])
        for i in range(heads):
            hd = slice(i * HEAD_DIM, (i + 1) * HEAD_DIM)
            dq[hd, qcols] = mm(kt_own[hd, :], ds[:, i * block:(i + 1) * block])

        def query_grad(i):
            ds_i = (s_far[i, b] * (g_far[i, b] - stat[b, 1:2])).astype(BF16)
            for j in range(heads):
                hd = slice(j * HEAD_DIM, (j + 1) * HEAD_DIM)
                dq[hd, qcols] += mm(kt_far[i, hd, qcols], ds_i[:, j * block:(j + 1) * block])

        query_grad(0)
        each(query_grad)

    def backward_slot(i):
        c0, c1 = rc[i, 0], rc[i, 1]
        g = (mm_nt(c0, w_o[:, :half]) + mm_nt(c1, w_o[:, half:])).astype(BF16)
        for b in range(2):
            here = slice(b * block, (b + 1) * block)
            gm = masked(g, b)
            row_total = stat_far[i, b, 0:1]
            dot = stat_far[i, b, 1:2]
            if isinstance(i, int) and i == 0:
                w = stat_far[i, b, 2:3]
            else:
                w = jnp.zeros((1, heads * block), F32) + far_weight(i, b)
            p = jnp.exp(s_back[i, b] - jnp.where(w > 0.0, row_total, -OFF)) * w
            gp = mm_nt(v_own[here, :], gm)
            ds = (p * (gp - dot)).astype(BF16)
            dv[here, :] += mm(p.astype(BF16), gm)
            dk[here, :] += mm(ds, qm_far[i, b])

    pass_on(c_slab, c_hop)
    for c in c_near():
        c.wait_recv()
    c_twin(0).start()
    c_twin(0).wait_recv()
    for c in stat_near():
        c.wait_recv()
    backward_slot(0)

    def take_c(d):
        arrive(c_slab, d)
        c_twin(d).start()
        c_twin(d).wait_recv()
        stat_slab(d).wait_recv()
        backward_slot(d)

    each(take_c)

    dq_low = (dq[...].T * scale).astype(BF16)
    dk_low, dv_low = dk[...].astype(BF16), dv[...].astype(BF16)

    def share(which):
        at = pl.ds(pl.multiple_of(which * half, half), half)
        return mm_nt(dq_low, w_q[at, :]) + mm_nt(dk_low, w_k[at, :]) + mm_nt(dv_low, w_v[at, :])

    give[...] = share(1 - h).astype(BF16)
    swap = copy(give, take, h_send, h_recv, twin)
    swap.start()
    mine = share(h)
    swap.wait_recv()
    branch = (mine + take[...].astype(F32)).astype(BF16)
    out[...] = mm(perm[...], branch).astype(BF16)

    swap.wait_send()
    for c in (*x_near(), *c_near(), *stat_near(), x_twin(0), c_twin(0)):
        c.wait_send()

    def finish(d):
        for c in (stat_slab(d), x_twin(d), c_twin(d)):
            c.wait_send()

    each(finish)
    each_direct(lambda d: x_slab(d).wait_send())
    each_direct(lambda d: c_slab(d).wait_send())
    if line:
        @pl.when(inner)
        def _():
            x_hop().wait_send()
            c_hop().wait_send()


def body(features, cotangent, w_query, w_key, w_value, w_out, adjacency, partner, node_order):
    n, nb = lax.axis_size("slab"), lax.axis_size("blk")
    rows, width = features.shape
    cols = w_query.shape[1]
    half, block = width // 2, rows // 2
    lanes = (cols // HEAD_DIM) * block
    vm, dma = pltpu.VMEM, pltpu.SemaphoreType.DMA
    vmem, hbm = (pl.BlockSpec(memory_space=m) for m in (pltpu.VMEM, pltpu.HBM))
    return pl.pallas_call(
        functools.partial(kernel, n, nb),
        out_shape=jax.ShapeDtypeStruct((rows, half), BF16),
        in_specs=[hbm] * 9,
        out_specs=vmem,
        scratch_shapes=[
            vm((rows, width), BF16), vm((rows, width), BF16),
            vm((width, cols), BF16), vm((width, cols), BF16), vm((width, cols), BF16),
            vm((cols, width), BF16), pltpu.SMEM(adjacency.shape, jnp.int32),
            pltpu.SMEM(adjacency.shape, jnp.int32), vm((1, rows), jnp.int32), dma((9,)),
            vm((rows, rows), BF16),
            vm((2, rows, half), BF16), vm((2, rows, half), BF16),
            vm((n, 2, rows, half), BF16), vm((n, 2, rows, half), BF16),
            vm((rows, cols), BF16), vm((rows, cols), BF16), vm((cols, rows), BF16),
            vm((2, lanes, cols), BF16), vm((2, lanes, cols), BF16),
            vm((n, cols, rows), BF16), vm((n, 2, lanes, cols), BF16),
            vm((2, rows, lanes), F32), vm((2, rows, lanes), F32),
            vm((n, 2, block, lanes), F32), vm((n, 2, block, lanes), F32),
            vm((n, 2, block, lanes), F32),
            vm((2, 1, lanes), F32), vm((2, 8, lanes), F32), vm((n, 2, 8, lanes), F32),
            vm((cols, rows), F32), vm((rows, cols), F32), vm((rows, cols), F32),
            vm((rows, half), BF16), vm((rows, half), BF16),
        ] + [dma((n + 1,)), dma((n + 1,)), dma((n,)), dma((n,))] * 2
        + [dma((n + 1,)), dma((n + 1,)), dma(()), dma(()), dma((2,))],
        compiler_params=pltpu.CompilerParams(
            collective_id=0, has_side_effects=True, vmem_limit_bytes=63 * 1024 * 1024
        ),
    )(
        features, cotangent, w_query, w_key, w_value, w_out,
        adjacency, partner.T, node_order.reshape(1, rows),
    )


def solution(mesh):
    rows = P(("parts", "slab", "blk"), None)
    in_specs = (
        rows, rows,
        P(None, "head"), P(None, "head"), P(None, "head"), P("head", None),
        rows, P(None, ("parts", "slab", "blk")), P(("parts", "slab", "blk")),
    )
    return jax.shard_map(
        body, mesh=mesh, in_specs=in_specs,
        out_specs=P(("parts", "slab", "blk"), "head"), check_vma=False,
    )
```

```python
import functools

import jax
import jax.numpy as jnp
from jax import lax
from jax.experimental import pallas as pl
from jax.experimental.pallas import tpu as pltpu
from jax.sharding import PartitionSpec as P

HEAD_DIM = 64
OFF = -1e30
NT = (((1,), (1,)), ((), ()))
TN = (((0,), (0,)), ((), ()))
F32, BF16 = jnp.float32, jnp.bfloat16
MESH = pl.DeviceIdType.MESH


def mm(a, b):
    return jnp.dot(a, b, preferred_element_type=F32)


def mm_nt(a, b):
    return lax.dot_general(a, b, NT, preferred_element_type=F32)


def kernel(
    n, nb,
    feat_hbm, cot_hbm, w_q_hbm, w_k_hbm, w_v_hbm, w_o_hbm, adj_hbm, part_hbm, order_hbm, out,
    feat, cot, w_q, w_k, w_v, w_o, adj, part, order, fetch,
    perm, own_x, own_c, rx, rc, k_own, v_own, kt_own, qm_own, gm_own,
    kt_far, qm_far, s_loc, g_loc, s_far, g_far, s_back, peak, stat, stat_far,
    dq, dk, dv, give, take,
    x_send, x_recv, xf_send, xf_recv, c_send, c_recv, cf_send, cf_recv,
    t_send, t_recv, h_send, h_recv, hop_send, part_out,
):
    rows, width = feat.shape
    half = width // 2
    cols = w_q.shape[1]
    heads = cols // HEAD_DIM
    block = rows // 2
    scale = HEAD_DIM ** -0.5
    h, slab, x = (lax.axis_index(a) for a in ("head", "slab", "blk"))
    behind, ahead = {"blk": lax.rem(x + nb - 1, nb)}, {"blk": lax.rem(x + 1, nb)}
    twin = {"head": 1 - h}

    def onward(d):
        return {"slab": lax.rem(slab + d, n)}

    line = n == 4
    at_start, at_end = slab == 0, slab == n - 1
    inner = jnp.logical_and(slab > 0, slab < n - 1)

    def each(f):
        if line:
            f(jnp.where(at_start, 3, 1))
            f(jnp.where(inner, 3, 2))
            f(jnp.where(at_start, 1, jnp.where(at_end, 3, 2)))
        elif n <= 4:
            for d in range(1, n):
                f(d)
        else:
            lax.fori_loop(1, n, lambda d, c: (f(d), c)[1], 0)

    def stream(arrived, twin_of, work):
        if line:
            order_of = [
                0, jnp.where(at_start, 3, 1), jnp.where(inner, 3, 2),
                jnp.where(at_start, 1, jnp.where(at_end, 3, 2)),
            ]
            arrived(0)
            twin_of(0).start()
            for at, now in enumerate(order_of):
                if at + 1 < n:
                    arrived(order_of[at + 1])
                    twin_of(order_of[at + 1]).start()
                twin_of(now).wait_recv()
                work(now)
        else:
            def step(d):
                arrived(d)
                twin_of(d).start()
                twin_of(d).wait_recv()
                work(d)

            step(0)
            each(step)

    def each_direct(f):
        if line:
            f(2)
            pl.when(jnp.logical_not(at_end))(lambda: f(1))
            pl.when(jnp.logical_not(at_start))(lambda: f(3))
        else:
            each(f)

    loads = [
        pltpu.make_async_copy(src, dst, fetch.at[i])
        for i, (src, dst) in enumerate((
            (order_hbm, order), (feat_hbm, feat), (cot_hbm, cot), (w_q_hbm, w_q), (w_k_hbm, w_k),
            (w_v_hbm, w_v), (w_o_hbm, w_o), (adj_hbm, adj), (part_hbm, part),
        ))
    ]
    for load in loads:
        load.start()
    barrier = pltpu.get_barrier_semaphore()

    def greet(where):
        pl.semaphore_signal(barrier, inc=1, device_id=where, device_id_type=MESH)

    greet(behind)
    greet(ahead)
    greet(twin)
    each(lambda d: greet(onward(d)))

    def copy(src, dst, send, recv, where):
        return pltpu.make_async_remote_copy(
            src_ref=src, dst_ref=dst, send_sem=send, recv_sem=recv,
            device_id=where, device_id_type=MESH,
        )

    low, high = pl.ds(0, block), pl.ds(block, block)

    def near_copies(own, far, send, recv):
        return (
            copy(own.at[h, low], far.at[0, h, high], send.at[n], recv.at[n], behind),
            copy(own.at[h, high], far.at[0, h, low], send.at[0], recv.at[0], ahead),
        )

    def slab_copy(own, far, send, recv, d):
        return copy(own.at[h], far.at[d, h], send.at[d], recv.at[d], onward(d))

    def twin_copy(far, send, recv, i):
        return copy(far.at[i, h], far.at[i, h], send.at[i], recv.at[i], twin)

    x_near = functools.partial(near_copies, own_x, rx, x_send, x_recv)
    c_near = functools.partial(near_copies, own_c, rc, c_send, c_recv)
    x_slab = functools.partial(slab_copy, own_x, rx, x_send, x_recv)
    c_slab = functools.partial(slab_copy, own_c, rc, c_send, c_recv)
    x_twin = functools.partial(twin_copy, rx, xf_send, xf_recv)
    c_twin = functools.partial(twin_copy, rc, cf_send, cf_recv)

    def hop_copy(far, recv, k):
        up = slab == n - 2
        slot = jnp.where(up, 3, 1)
        return copy(
            far.at[2, h], far.at[slot, h], hop_send.at[k], recv.at[slot],
            {"slab": jnp.where(up, n - 1, 0)},
        )

    x_hop = functools.partial(hop_copy, rx, x_recv, 0)
    c_hop = functools.partial(hop_copy, rc, c_recv, 1)

    def pass_on(slab_copy_of, hop):
        if line:
            @pl.when(inner)
            def _():
                slab_copy_of(2).wait_recv()
                hop().start()

    def arrive(slab_copy_of, d):
        if line:
            pl.when(jnp.logical_not(jnp.logical_and(inner, d == 2)))(
                lambda: slab_copy_of(d).wait_recv()
            )
        else:
            slab_copy_of(d).wait_recv()

    def stat_near():
        return (
            copy(stat.at[0], stat_far.at[0, 1], t_send.at[n], t_recv.at[n], behind),
            copy(stat.at[1], stat_far.at[0, 0], t_send.at[0], t_recv.at[0], ahead),
        )

    def stat_slab(d):
        return copy(stat, stat_far.at[d], t_send.at[d], t_recv.at[d], onward(d))

    loads[0].wait()
    loads[1].wait()
    hot = lax.broadcasted_iota(jnp.int32, (rows, rows), 0) == order[...]
    perm[...] = jnp.where(hot, 1.0, 0.0).astype(BF16)
    x_all = lax.dot_general(perm[...], feat[...], TN, preferred_element_type=F32).astype(BF16)
    own_x[0] = x_all[:, :half]
    own_x[1] = x_all[:, half:]

    for load in loads[2:]:
        load.wait()
    c_all = lax.dot_general(perm[...], cot[...], TN, preferred_element_type=F32).astype(BF16)
    own_c[0] = c_all[:, :half]
    own_c[1] = c_all[:, half:]

    lane_head = lax.broadcasted_iota(jnp.int32, (1, cols), 1) // HEAD_DIM
    masks = [jnp.where(lane_head == i, 1.0, 0.0).astype(BF16) for i in range(heads)]

    def masked(value, b):
        part_rows = value[b * block:(b + 1) * block]
        return jnp.concatenate([part_rows * mask for mask in masks], axis=0)

    def weight_flag(flag):
        return jnp.where(flag > 0, 1.0, 0.0).astype(F32)

    def far_weight(i, b):
        if isinstance(i, int) and i == 0:
            return weight_flag(adj[0, 0] if b == 0 else adj[1, 2])
        source = lax.rem(slab + n - i, n)
        total = jnp.float32(0.0)
        for m in range(3):
            total = total + jnp.where(lax.div(part[b, m], 2 * nb) == source, 1.0, 0.0)
        return total

    def local_weight(kb, qb):
        if kb == qb:
            return jnp.float32(1.0)
        return weight_flag(adj[0, 2] if qb == 0 else adj[1, 0])

    def bias(w):
        return jnp.where(w > 0.0, 0.0, OFF).astype(F32)

    q_all = (mm(x_all, w_q[...]).astype(BF16) * scale).astype(BF16)
    k_all = mm(x_all, w_k[...])
    k_own[...] = k_all.astype(BF16)
    kt_own[...] = k_all.T.astype(BF16)
    v_own[...] = mm(x_all, w_v[...]).astype(BF16)
    g_all = mm_nt(c_all, w_o[...]).astype(BF16)
    for b in range(2):
        qm_own[b] = masked(q_all, b)
        gm_own[b] = masked(g_all, b)
    pl.semaphore_wait(barrier, n + 2)
    for c in x_near():
        c.start()
    each_direct(lambda d: x_slab(d).start())
    for b in range(2):
        s = mm_nt(k_own[...], qm_own[b])
        s_loc[b] = s
        g_loc[b] = mm_nt(v_own[...], gm_own[b])
        top = [
            jnp.max(s[kb * block:(kb + 1) * block], axis=0, keepdims=True)
            + bias(local_weight(kb, b))
            for kb in range(2)
        ]
        peak[b] = jnp.maximum(top[0], top[1])

    def forward_slot(i):
        x0, x1 = rx[i, 0], rx[i, 1]

        def project(w):
            return mm(x0, w[:half, :]) + mm(x1, w[half:, :])

        q = (project(w_q).astype(BF16) * scale).astype(BF16)
        k32 = project(w_k)
        k = k32.astype(BF16)
        kt_far[i] = k32.T.astype(BF16)
        v = project(w_v).astype(BF16)
        for b in range(2):
            here = slice(b * block, (b + 1) * block)
            qm = masked(q, b)
            qm_far[i, b] = qm
            s = mm_nt(k[here], qm_own[b])
            s_far[i, b] = s
            g_far[i, b] = mm_nt(v[here], gm_own[b])
            s_back[i, b] = mm_nt(k_own[here, :], qm)
            top = jnp.max(s, axis=0, keepdims=True) + bias(far_weight(i, b))
            peak[b] = jnp.maximum(peak[b], top)

    pass_on(x_slab, x_hop)
    def x_arrived(d):
        if isinstance(d, int) and d == 0:
            for c in x_near():
                c.wait_recv()
        else:
            arrive(x_slab, d)

    def forward_step(i):
        forward_slot(i)
        if isinstance(i, int) and i == 0:
            for c in c_near():
                c.start()
            each_direct(lambda d: c_slab(d).start())

    stream(x_arrived, x_twin, forward_step)

    for b in range(2):
        qcols = slice(b * block, (b + 1) * block)
        top = peak[b]

        def expo(ref, at, w, total):
            e = jnp.exp(ref[at] + (bias(w) - top))
            ref[at] = e
            return total + w * jnp.sum(e, axis=0, keepdims=True)

        def loc(kb):
            return (b, slice(kb * block, (kb + 1) * block))

        total = jnp.zeros((1, heads * block), F32)
        for kb in range(2):
            total = expo(s_loc, loc(kb), local_weight(kb, b), total)
        total = expo(s_far, (0, b), far_weight(0, b), total)
        stat[b, 0:1] = total

        def far_expo(d):
            stat[b, 0:1] = expo(s_far, (d, b), far_weight(d, b), stat[b, 0:1])

        each(far_expo)
        total = stat[b, 0:1]
        inverse = 1.0 / total

        def weigh(sref, gref, at, w):
            p = sref[at] * (w * inverse)
            sref[at] = p
            low_p = p.astype(BF16).astype(F32)
            return jnp.sum(low_p * gref[at], axis=0, keepdims=True)

        dot = weigh(s_far, g_far, (0, b), far_weight(0, b))
        for kb in range(2):
            dot = dot + weigh(s_loc, g_loc, loc(kb), local_weight(kb, b))
        stat[b, 1:2] = dot

        def far_weigh(d):
            stat[b, 1:2] = stat[b, 1:2] + weigh(s_far, g_far, (d, b), far_weight(d, b))

        each(far_weigh)
        stat[b, 0:1] = top + jnp.log(total)
        flag = weight_flag(adj[0, 0] if b == 0 else adj[1, 2])
        stat[b, 2:3] = jnp.zeros((1, heads * block), F32) + flag
        stat[b, 3:8] = jnp.zeros((5, heads * block), F32)
    for c in stat_near():
        c.start()
    each(lambda d: stat_slab(d).start())

    for b in range(2):
        qcols = slice(b * block, (b + 1) * block)
        dot = stat[b, 1:2]
        p = s_loc[b]
        ds = (p * (g_loc[b] - dot)).astype(BF16)
        p_low = p.astype(BF16)
        if b == 0:
            dv[...] = mm(p_low, gm_own[b])
            dk[...] = mm(ds, qm_own[b])
        else:
            dv[...] += mm(p_low, gm_own[b])
            dk[...] += mm(ds, qm_own[b])
        for i in range(heads):
            hd = slice(i * HEAD_DIM, (i + 1) * HEAD_DIM)
            dq[hd, qcols] = mm(kt_own[hd, :], ds[:, i * block:(i + 1) * block])

        def query_grad(i):
            ds_i = (s_far[i, b] * (g_far[i, b] - stat[b, 1:2])).astype(BF16)
            for j in range(heads):
                hd = slice(j * HEAD_DIM, (j + 1) * HEAD_DIM)
                dq[hd, qcols] += mm(kt_far[i, hd, qcols], ds_i[:, j * block:(j + 1) * block])

        query_grad(0)
        each(query_grad)

    def backward_slot(i):
        c0, c1 = rc[i, 0], rc[i, 1]
        g = (mm_nt(c0, w_o[:, :half]) + mm_nt(c1, w_o[:, half:])).astype(BF16)
        for b in range(2):
            here = slice(b * block, (b + 1) * block)
            gm = masked(g, b)
            row_total = stat_far[i, b, 0:1]
            dot = stat_far[i, b, 1:2]
            if isinstance(i, int) and i == 0:
                w = stat_far[i, b, 2:3]
            else:
                w = jnp.zeros((1, heads * block), F32) + far_weight(i, b)
            p = jnp.exp(s_back[i, b] - jnp.where(w > 0.0, row_total, -OFF)) * w
            gp = mm_nt(v_own[here, :], gm)
            ds = (p * (gp - dot)).astype(BF16)
            dv[here, :] += mm(p.astype(BF16), gm)
            dk[here, :] += mm(ds, qm_far[i, b])

    pass_on(c_slab, c_hop)
    def c_arrived(d):
        if isinstance(d, int) and d == 0:
            for c in (*c_near(), *stat_near()):
                c.wait_recv()
        else:
            arrive(c_slab, d)
            stat_slab(d).wait_recv()

    dq_low = (dq[...].T * scale).astype(BF16)

    def half_at(which):
        return pl.ds(pl.multiple_of(which * half, half), half)

    for k, which in enumerate((1 - h, h)):
        part_out[k] = mm_nt(dq_low, w_q[half_at(which), :])
    stream(c_arrived, c_twin, backward_slot)

    dk_low, dv_low = dk[...].astype(BF16), dv[...].astype(BF16)

    def share(k, which):
        at = half_at(which)
        return part_out[k] + mm_nt(dk_low, w_k[at, :]) + mm_nt(dv_low, w_v[at, :])

    give[...] = share(0, 1 - h).astype(BF16)
    swap = copy(give, take, h_send, h_recv, twin)
    swap.start()
    mine = share(1, h)
    swap.wait_recv()
    branch = (mine + take[...].astype(F32)).astype(BF16)
    out[...] = mm(perm[...], branch).astype(BF16)

    swap.wait_send()
    for c in (*x_near(), *c_near(), *stat_near(), x_twin(0), c_twin(0)):
        c.wait_send()

    def finish(d):
        for c in (stat_slab(d), x_twin(d), c_twin(d)):
            c.wait_send()

    each(finish)
    each_direct(lambda d: x_slab(d).wait_send())
    each_direct(lambda d: c_slab(d).wait_send())
    if line:
        @pl.when(inner)
        def _():
            x_hop().wait_send()
            c_hop().wait_send()


def body(features, cotangent, w_query, w_key, w_value, w_out, adjacency, partner, node_order):
    n, nb = lax.axis_size("slab"), lax.axis_size("blk")
    rows, width = features.shape
    cols = w_query.shape[1]
    half, block = width // 2, rows // 2
    lanes = (cols // HEAD_DIM) * block
    vm, dma = pltpu.VMEM, pltpu.SemaphoreType.DMA
    vmem, hbm = (pl.BlockSpec(memory_space=m) for m in (pltpu.VMEM, pltpu.HBM))
    return pl.pallas_call(
        functools.partial(kernel, n, nb),
        out_shape=jax.ShapeDtypeStruct((rows, half), BF16),
        in_specs=[hbm] * 9,
        out_specs=vmem,
        scratch_shapes=[
            vm((rows, width), BF16), vm((rows, width), BF16),
            vm((width, cols), BF16), vm((width, cols), BF16), vm((width, cols), BF16),
            vm((cols, width), BF16), pltpu.SMEM(adjacency.shape, jnp.int32),
            pltpu.SMEM(adjacency.shape, jnp.int32), vm((1, rows), jnp.int32), dma((9,)),
            vm((rows, rows), BF16),
            vm((2, rows, half), BF16), vm((2, rows, half), BF16),
            vm((n, 2, rows, half), BF16), vm((n, 2, rows, half), BF16),
            vm((rows, cols), BF16), vm((rows, cols), BF16), vm((cols, rows), BF16),
            vm((2, lanes, cols), BF16), vm((2, lanes, cols), BF16),
            vm((n, cols, rows), BF16), vm((n, 2, lanes, cols), BF16),
            vm((2, rows, lanes), F32), vm((2, rows, lanes), F32),
            vm((n, 2, block, lanes), F32), vm((n, 2, block, lanes), F32),
            vm((n, 2, block, lanes), F32),
            vm((2, 1, lanes), F32), vm((2, 8, lanes), F32), vm((n, 2, 8, lanes), F32),
            vm((cols, rows), F32), vm((rows, cols), F32), vm((rows, cols), F32),
            vm((rows, half), BF16), vm((rows, half), BF16),
        ] + [dma((n + 1,)), dma((n + 1,)), dma((n,)), dma((n,))] * 2
        + [dma((n + 1,)), dma((n + 1,)), dma(()), dma(()), dma((2,)), vm((2, rows, half), F32)],
        compiler_params=pltpu.CompilerParams(
            collective_id=0, has_side_effects=True, vmem_limit_bytes=63 * 1024 * 1024
        ),
    )(
        features, cotangent, w_query, w_key, w_value, w_out,
        adjacency, partner.T, node_order.reshape(1, rows),
    )


def solution(mesh):
    rows = P(("parts", "slab", "blk"), None)
    in_specs = (
        rows, rows,
        P(None, "head"), P(None, "head"), P(None, "head"), P("head", None),
        rows, P(None, ("parts", "slab", "blk")), P(("parts", "slab", "blk")),
    )
    return jax.shard_map(
        body, mesh=mesh, in_specs=in_specs,
        out_specs=P(("parts", "slab", "blk"), "head"), check_vma=False,
    )
```
